512 devices in a mesh: tok: 128 (over y, z_lo, x, core), head: 4 (over z_hi).
Axes of the slice: x: 4, y: 4, z: 16 (z_hi: 4, z_lo: 4; z = z_hi * 4 + z_lo), core: 2. Of those that a mesh axis runs over, the one named last changes fastest.
Arguments:
- fast_query: bfloat16 [2, 16384, 2048], P(None, 'tok', 'head'), may hold values from -6 to 6
- fast_key: bfloat16 [2, 16384, 2048], P(None, 'tok', 'head'), may hold values from -6 to 6
- fast_value: bfloat16 [2, 16384, 2048], P(None, 'tok', 'head'), may hold values from -6 to 6
- fast_rate: float32 [2, 16384, 4], P(None, 'tok', 'head'), may hold values from 0.00078125 to 0.0078125
- fast_weights: bfloat16 [4, 512, 3, 512], P('head', 'tok'), may hold values from -0.25 to 0.25
- norm_gain: float32 [2048], P('head'), may hold values from 0.25 to 1.75
- key_value: bfloat16 [2, 16384, 512], P(None, 'tok', 'head'), may hold values from -450 to 450
Outputs:
- layer_output: bfloat16 [2, 16384, 2048], P(None, 'tok', 'head')
The draws below stay inside these ranges and needn't reach their ends.
All inputs are finite; a program needn't handle non-finite values.
Results may differ from the reference program's by a relative error of at most 0.04.
The reference program's roundings to bfloat16 on the way count: a program that leaves them out, or rounds other values in their place, can miss the bound.
Values may be sent and summed in bfloat16 or wider, within the bound.
No kernel may reach another device: no remote copies, remote signals or barrier semaphores. Data moves between devices by JAX's collectives and lax.ppermute only.
A program may use at most 64 MiB of HBM per device.

```python
import math
import jax
import jax.numpy as jnp
from jax import lax

D = 2048
FWH = 4
HD = 512
FH = 512
QH = 16
KVH = 2
AD = 128
WIN = 1024
BLOCK = 16384


def draw_key_value(key, part):
    key_base = jax.random.fold_in(key, 0)
    key_other = jax.random.fold_in(key, 3)
    columns = 2 * KVH * AD
    column_block = jnp.arange(columns) // AD
    is_key = column_block % 2 == 0
    key_rows = 2.0 * jnp.clip(jax.random.normal(key_base, (2, BLOCK, columns), jnp.float32), -5.0, 5.0)
    value_rows = 3.0 * jnp.clip(jax.random.normal(key_other, (2, BLOCK, columns), jnp.float32), -5.0, 5.0)
    return jnp.where(is_key, key_rows, value_rows).astype(jnp.bfloat16)


def steps_of(stream_key, dims, cuts, smallest, top_value):
    level = 1.0
    for dim, parts in cuts:
        draws = jax.random.uniform(jax.random.fold_in(jax.random.fold_in(stream_key, 6), dim), (parts,), jnp.float32, smallest / len(cuts), top_value / len(cuts))
        level = level * jnp.repeat(jnp.exp(draws), dims[dim] // parts).reshape((-1,) + (1,) * (len(dims) - 1 - dim))
    return level


def gaussian(key, shape, scale, reach, pieces=(), held_as=jnp.bfloat16):
    drawn = scale * jax.random.normal(key, shape, jnp.float32)
    if pieces:
        drawn = drawn * steps_of(key, shape, pieces, -0.22, 0.18)
    return jnp.clip(drawn, -reach, reach).astype(held_as)


def setup_inputs(seed: int = 0) -> dict:
    key_of = jax.random.split(jax.random.key(seed), 8)
    fast_query = gaussian(key_of[0], (2, BLOCK, D), 1.0, 6.0, ((1, 128), (2, 4)))
    fast_key = gaussian(key_of[1], (2, BLOCK, D), 1.0, 6.0, ((1, 128), (2, 4)))
    fast_value = gaussian(key_of[2], (2, BLOCK, D), 1.0, 6.0, ((1, 128), (2, 4)))
    fast_rate = jnp.clip(jnp.exp(math.log(0.0078125) - 2.3025851 * jax.random.uniform(key_of[3], (2, BLOCK, FWH), jnp.float32) ** steps_of(key_of[3], (2, BLOCK, FWH), ((1, 128), (2, 4)), -0.2, 0.2)), 0.00078125, 0.0078125)
    fast_weights = gaussian(key_of[4], (FWH, HD, 3, FH), HD ** -0.5, 0.25, ((0, 4), (1, 128)))
    norm_gain = jnp.clip(1.0 + 0.15 * jax.random.normal(key_of[5], (D,), jnp.float32), 0.25, 1.75)
    key_value = draw_key_value(jax.random.fold_in(key_of[7], 71), 0)
    return {"fast_query": fast_query, "fast_key": fast_key, "fast_value": fast_value, "fast_rate": fast_rate, "fast_weights": fast_weights, "norm_gain": norm_gain, "key_value": key_value}


EPSILON = 1e-06

def fast_apply(inputs, weights):
    gate_value = jnp.dot(inputs, weights[:, 0], preferred_element_type=jnp.float32)
    up_value = jnp.dot(inputs, weights[:, 1], preferred_element_type=jnp.float32)
    hidden = (jax.nn.silu(gate_value) * up_value).astype(jnp.bfloat16)
    return jnp.dot(hidden, weights[:, 2], preferred_element_type=jnp.float32)

def renormed(previous, gradient):
    earlier = previous.astype(jnp.float32)
    updated = earlier + gradient
    factor = jnp.sqrt(lax.optimization_barrier(jnp.mean(earlier * earlier, axis=-1, keepdims=True)) + EPSILON) * lax.rsqrt(lax.optimization_barrier(jnp.mean(updated * updated, axis=-1, keepdims=True)) + EPSILON)
    return (updated * factor).astype(jnp.bfloat16)

def normalized(raw, gain_row):
    factor = lax.rsqrt(lax.optimization_barrier(jnp.mean(raw * raw, axis=-1, keepdims=True)) + EPSILON)
    return (raw * factor * gain_row).astype(jnp.bfloat16)

def head_output(inputs):
    query_in, key_in, value_in, rate_in, weights, gain_row = inputs
    key_first = key_in[0]
    gate_value = jnp.dot(key_first, weights[:, 0], preferred_element_type=jnp.float32)
    up_value = jnp.dot(key_first, weights[:, 1], preferred_element_type=jnp.float32)
    sigmoid_gate = jax.nn.sigmoid(gate_value)
    activated = gate_value * sigmoid_gate
    key_hidden = (activated * up_value).astype(jnp.bfloat16)
    scaled = (rate_in[0] * value_in[0].astype(jnp.float32)).astype(jnp.bfloat16)
    backward = jnp.dot(scaled, weights[:, 2].T, preferred_element_type=jnp.float32)
    gate_grad = (backward * up_value * sigmoid_gate * (1.0 + gate_value * (1.0 - sigmoid_gate))).astype(jnp.bfloat16)
    up_grad = (backward * activated).astype(jnp.bfloat16)
    gradient = jnp.stack([jnp.dot(key_first.T, gate_grad, preferred_element_type=jnp.float32), jnp.dot(key_first.T, up_grad, preferred_element_type=jnp.float32), jnp.dot(key_hidden.T, scaled, preferred_element_type=jnp.float32)], axis=1)
    refreshed = renormed(weights, gradient)
    first_out = normalized(fast_apply(query_in[0], weights), gain_row)
    second_out = normalized(fast_apply(query_in[1], refreshed), gain_row)
    return jnp.stack([first_out, second_out])

def attention_head(queries, key_cols, value_cols):
    total_len = queries.shape[0]
    query_block = min(512, total_len // 2)
    lead = jnp.zeros((WIN, key_cols.shape[1]), key_cols.dtype)
    keys_padded = jnp.concatenate([lead, key_cols], axis=0)
    values_padded = jnp.concatenate([lead, value_cols], axis=0)

    def one_block(block_start):
        query_part = lax.dynamic_slice_in_dim(queries, block_start, query_block, 0)
        key_part = lax.dynamic_slice_in_dim(keys_padded, block_start, query_block + WIN, 0)
        value_part = lax.dynamic_slice_in_dim(values_padded, block_start, query_block + WIN, 0)
        scores = jnp.dot(query_part, key_part.T, preferred_element_type=jnp.float32) / math.sqrt(key_cols.shape[1])
        query_pos = block_start + lax.broadcasted_iota(jnp.int32, scores.shape, 0)
        key_pos = block_start - WIN + lax.broadcasted_iota(jnp.int32, scores.shape, 1)
        offset = query_pos - key_pos
        allowed = (key_pos >= 0) & (offset >= 0) & (offset < WIN)
        scores = jnp.where(allowed, scores, -1e+30)
        row_max = lax.optimization_barrier(jnp.max(scores, axis=-1, keepdims=True))
        lifted = jnp.exp(scores - row_max)
        weights = (lifted / lax.optimization_barrier(jnp.sum(lifted, axis=-1, keepdims=True))).astype(jnp.bfloat16)
        return jnp.dot(weights, value_part, preferred_element_type=jnp.float32)
    starts = jnp.arange(total_len // query_block, dtype=jnp.int32) * query_block
    return lax.map(one_block, starts).reshape(total_len, key_cols.shape[1])

def reference(fast_query, fast_key, fast_value, fast_rate, fast_weights, norm_gain, key_value):

    def split_heads(array):
        return jnp.moveaxis(array.reshape(2, BLOCK, FWH, HD), 2, 0)
    rates = jnp.moveaxis(fast_rate, 2, 0)[..., None]
    gains = norm_gain.reshape(FWH, HD)
    fast_out = lax.map(head_output, (split_heads(fast_query), split_heads(fast_key), split_heads(fast_value), rates, fast_weights, gains))
    fast_out = jnp.moveaxis(fast_out, 0, 2).reshape(2 * BLOCK, D)
    flat_kv = key_value.reshape(2 * BLOCK, 2 * KVH * AD)
    group = QH // KVH

    def one_query_head(head_index):
        queries = lax.dynamic_slice_in_dim(fast_out, (head_index * AD).astype(jnp.int32), AD, 1)
        kv_index = head_index // group
        key_cols = lax.dynamic_slice_in_dim(flat_kv, (2 * kv_index * AD).astype(jnp.int32), AD, 1)
        value_cols = lax.dynamic_slice_in_dim(flat_kv, ((2 * kv_index + 1) * AD).astype(jnp.int32), AD, 1)
        return attention_head(queries, key_cols, value_cols)
    mixed = lax.map(one_query_head, jnp.arange(QH, dtype=jnp.int32))
    attended = jnp.moveaxis(mixed, 0, 1).reshape(2 * BLOCK, D)
    total = (fast_out.astype(jnp.float32) + attended).astype(jnp.bfloat16)
    return total.reshape(2, BLOCK, D)
```

```python
import math

import jax
import jax.numpy as jnp
from jax import lax
from jax.sharding import Mesh, PartitionSpec as P

WIN = 1024
EPSILON = 1e-06
TOK = ("y", "z", "x", "c")
PLANE = ("y", "x")


def product(inputs, matrix):
    return jnp.dot(inputs, matrix, preferred_element_type=jnp.float32)


def order_matrix(width):
    sizes = [lax.axis_size(axis) for axis in TOK]
    ny, nz, nx, nc = sizes
    nj = width // (ny * nz * nx * nc)
    place = lax.broadcasted_iota(jnp.int32, (width, width), 1)
    j = place % nj
    z = place // nj % nz
    x = place // (nj * nz) % nx
    y = place // (nj * nz * nx) % ny
    c = place // (nj * nz * nx * ny)
    natural = (((y * nz + z) * nx + x) * nc + c) * nj + j
    return (natural == lax.broadcasted_iota(jnp.int32, (width, width), 0)).astype(jnp.bfloat16)


def exchange(array, axes):
    return lax.all_to_all(array, axes, 0, 0)


def to_all(array, axes):
    count = lax.axis_size(axes)
    return exchange(jnp.broadcast_to(array[None], (count,) + array.shape), axes)


def other_core(array):
    return lax.ppermute(array, "c", [(0, 1), (1, 0)])


def halves(array, core):
    half = array.shape[1] // 2
    first, second = array[:, :half], array[:, half:]
    return jnp.where(core == 0, first, second), jnp.where(core == 0, second, first)


def against(pair, own, other, low, high):
    return product(pair[0], own[:, low:high]) + product(pair[1], other[:, low:high])


def fast_apply(pair, own, other, core, width):
    gate_value = against(pair, own, other, 0, width)
    up_value = against(pair, own, other, width, 2 * width)
    hidden = (jax.nn.silu(gate_value) * up_value).astype(jnp.bfloat16)
    return against(halves(hidden, core), own, other, 2 * width, 3 * width)


def gradient(pair, value_in, rates, own, other, core, width):
    gate_value = against(pair, own, other, 0, width)
    up_value = against(pair, own, other, width, 2 * width)
    sigmoid_gate = jax.nn.sigmoid(gate_value)
    activated = gate_value * sigmoid_gate
    key_hidden = (activated * up_value).astype(jnp.bfloat16)
    scaled = (rates * value_in.astype(jnp.float32)).astype(jnp.bfloat16)
    along = (((1,), (1,)), ((), ()))
    back_own = lax.dot_general(scaled, own[:, 2 * width:], along, preferred_element_type=jnp.float32)
    back_other = lax.dot_general(scaled, other[:, 2 * width:], along, preferred_element_type=jnp.float32)
    backward = jnp.concatenate(
        [jnp.where(core == 0, back_own, back_other), jnp.where(core == 0, back_other, back_own)], axis=1
    )
    gate_grad = (
        backward * up_value * sigmoid_gate * (1.0 + gate_value * (1.0 - sigmoid_gate))
    ).astype(jnp.bfloat16)
    up_grad = (backward * activated).astype(jnp.bfloat16)
    across = (((0,), (0,)), ((), ()))
    hidden_pair = halves(key_hidden, core)

    def rows(which):
        return jnp.concatenate([
            lax.dot_general(pair[which], gate_grad, across, preferred_element_type=jnp.float32),
            lax.dot_general(pair[which], up_grad, across, preferred_element_type=jnp.float32),
            lax.dot_general(hidden_pair[which], scaled, across, preferred_element_type=jnp.float32),
        ], axis=1)

    return rows(0), rows(1).astype(jnp.bfloat16)


def renormed(previous, total, width):
    count = previous.shape[0]
    earlier = previous.astype(jnp.float32).reshape(count, 3, width)
    updated = earlier + total.reshape(count, 3, width)
    factor = jnp.sqrt(jnp.mean(earlier * earlier, axis=-1, keepdims=True) + EPSILON) * lax.rsqrt(
        jnp.mean(updated * updated, axis=-1, keepdims=True) + EPSILON
    )
    return (updated * factor).astype(jnp.bfloat16).reshape(count, 3 * width)


def normalized(raw, gain_row):
    factor = lax.rsqrt(jnp.mean(raw * raw, axis=-1, keepdims=True) + EPSILON)
    return (raw * factor * gain_row).astype(jnp.bfloat16)


def attend(queries, key_block, value_block, allowed, head_size):
    tokens = queries.shape[0]
    per_head = queries.reshape(tokens, -1, head_size)
    scores = jnp.einsum(
        "qhd,kd->hqk", per_head, key_block, preferred_element_type=jnp.float32
    ) / math.sqrt(head_size)
    scores = jnp.where(allowed[None], scores, -1e30)
    row_max = jnp.max(scores, axis=-1, keepdims=True)
    lifted = jnp.exp(scores - row_max)
    weights = (lifted / jnp.sum(lifted, axis=-1, keepdims=True)).astype(jnp.bfloat16)
    mixed = jnp.einsum("hqk,kd->qhd", weights, value_block, preferred_element_type=jnp.float32)
    return mixed.reshape(tokens, -1)


def passed_along(array, by):
    length = lax.axis_size(TOK)
    return lax.ppermute(array, TOK, [(i, (i + by) % length) for i in range(length)])


def preceding(key_value, place, reach):
    count = lax.axis_size("head")
    partner = lax.ppermute(key_value, "head", [(i, i ^ 1) for i in range(count)])
    holds_key = lax.axis_index("head") % 2 == 0
    pair = jnp.stack([jnp.where(holds_key, key_value, partner), jnp.where(holds_key, partner, key_value)])
    runs = [pair]
    step = 1
    while len(runs) < reach + 1:
        part = jnp.stack(runs[:step])
        for k in (1, 2):
            if len(runs) < reach + 1:
                moved = passed_along(part, k * step)
                runs += [moved[i] for i in range(step)]
        step = len(runs)
    aligned = []
    for distance in range(reach, 0, -1):
        piece = runs[distance]
        aligned.append(jnp.where(place >= distance, piece, piece[:, 0:1]))
    aligned.append(pair)
    return jnp.concatenate(aligned, axis=2)


def shards(fast_query, fast_key, fast_value, fast_rate, fast_weights, norm_gain, key_value):
    tokens, width = fast_query.shape[1:]
    head_size = key_value.shape[2]
    place = lax.axis_index(TOK)
    core = lax.axis_index("c")
    block_len = tokens * lax.axis_size(TOK)
    reach = WIN // tokens

    order = order_matrix(width)

    def reordered(array):
        return product(array, order).astype(jnp.bfloat16)

    rows = fast_weights[0]
    count = rows.shape[0]
    sides = reordered(rows[:, :2].reshape(2 * count, width)).reshape(count, 2 * width)
    own_rows = jnp.concatenate([sides, rows[:, 2]], axis=1)
    base = to_all(own_rows, "z").reshape(-1, 3 * width)
    own = to_all(base, PLANE).reshape(-1, 3 * width)
    other = other_core(own)

    window = preceding(key_value, place, reach)

    mine, theirs = gradient(
        halves(reordered(fast_key[0]), core), fast_value[0], fast_rate[0], own, other, core, width
    )
    chip_sum = (mine + other_core(theirs).astype(jnp.float32)).astype(jnp.bfloat16)
    pieces = exchange(chip_sum.reshape((-1,) + base.shape), PLANE)
    plane_sum = jnp.sum(pieces.astype(jnp.float32), axis=0).astype(jnp.bfloat16)
    total = jnp.sum(to_all(plane_sum, "z").astype(jnp.float32), axis=0)
    new_rows = renormed(base, total, width)
    new_own = to_all(new_rows, PLANE).reshape(-1, 3 * width)
    new_other = other_core(new_own)

    span = window.shape[2]
    query_pos = lax.broadcasted_iota(jnp.int32, (tokens, span), 0)
    key_pos = lax.broadcasted_iota(jnp.int32, (tokens, span), 1) - reach * tokens
    offset = query_pos - key_pos
    inside = (offset >= 0) & (offset < WIN)

    def finish(block_index, matrices):
        pair = halves(reordered(fast_query[block_index]), core)
        fast_out = normalized(fast_apply(pair, *matrices, core, width), norm_gain)
        allowed = inside & (block_index * block_len + place * tokens + key_pos >= 0)
        attended = attend(fast_out, window[0, block_index], window[1, block_index], allowed, head_size)
        return (fast_out.astype(jnp.float32) + attended).astype(jnp.bfloat16)

    return jnp.stack([finish(0, (own, other)), finish(1, (new_own, new_other))])


def solution(mesh):
    heads = mesh.shape["head"]
    fine = Mesh(mesh.devices.reshape(4, 4, 4, 2, heads), TOK + ("head",))
    in_specs = (
        P(None, TOK, "head"),
        P(None, TOK, "head"),
        P(None, TOK, "head"),
        P(None, TOK, "head"),
        P("head", TOK, None, None),
        P("head"),
        P(None, TOK, "head"),
    )
    out_specs = P(None, TOK, "head")
    return jax.shard_map(shards, mesh=fine, in_specs=in_specs, out_specs=out_specs, check_vma=False)
```
